256 devices in a mesh: row: 32 (over x, y, z_lo), src: 8 (over z_hi, core).
Axes of the slice: x: 4, y: 4, z: 8 (z_hi: 4, z_lo: 2; z = z_hi * 2 + z_lo), core: 2. Of those that a mesh axis runs over, the one named last changes fastest.
Arguments:
- traces: bfloat16 [16384, 128, 512], P('row', 'src'), may hold values from -6 to 6
- row_source: int32 [16384], P('row'), may hold values from 0 to 16383, as said below
- slice_data: bfloat16 [2, 16384, 32, 512], P(None, 'row', None, 'src'), may hold values from -0.03125 to 0.03125
- wavelet_inverse: float32 [2], replicated, may hold values from 0.3 to 0.8
Outputs:
- multiples: float32 [16384, 2, 128], P(('row', 'src'))
- primaries: float32 [16384, 2, 128], P(('row', 'src'))
The draws below stay inside these ranges and needn't reach their ends.
Inputs may be any that keep to these rules, and one draw needn't show every extreme that they name: `row_source`: every recording row is named exactly once; entry e * 512 + p names a recording row whose index modulo 512 lies in [e * 16, (e + 1) * 16).
All inputs are finite; a program needn't handle non-finite values.
Results may differ from the reference program's by a relative error of at most 0.0056.
Values may be sent and summed in bfloat16 or wider, within the bound.
A program may use at most 64 MiB of HBM per device.

```python
import jax
import jax.numpy as jnp

M = 16384
PC = 128
NT = 512
FREQ = 61
ITERS = 3
N_ROW = 32


def draw_row_source(key, part):
    block_rows = M // N_ROW
    group_rows = block_rows // N_ROW
    subkeys = jax.random.split(key, N_ROW)
    shuffles = jax.vmap(lambda subkey: jax.random.permutation(subkey, block_rows))(subkeys)
    flat_order = shuffles.reshape(-1).astype(jnp.int32)
    target = jnp.arange(M, dtype=jnp.int32) // block_rows
    return (flat_order // group_rows * block_rows + target * group_rows + flat_order % group_rows).astype(jnp.int32)


def level_of(key, extent, cuts, smallest, high):
    gain, own = 1.0, jax.random.fold_in(key, 6)
    for position, shards_of in cuts:
        draws = jnp.exp(jax.random.uniform(jax.random.fold_in(own, position), (shards_of,), jnp.float32, smallest / len(cuts), high / len(cuts)))
        gain = gain * jnp.repeat(draws, extent[position] // shards_of).reshape([-1 if axis == position else 1 for axis in range(len(extent))])
    return gain


def noise(key, dims, spread, reach, shards=(), held_as=jnp.bfloat16):
    entries = spread * jax.random.normal(key, dims, jnp.float32)
    if shards:
        entries = entries * level_of(key, dims, shards, -0.22, 0.18)
    return jnp.clip(entries, -reach, reach).astype(held_as)


def setup_inputs(seed: int = 0) -> dict:
    arg_keys = jax.random.split(jax.random.key(seed), 5)
    return {
        "traces": noise(arg_keys[0], (M, PC, NT), 1.0, 6.0, ((0, 32), (1, 8))),
        "row_source": draw_row_source(jax.random.fold_in(arg_keys[4], 71), 0),
        "slice_data": noise(arg_keys[2], (2, M, N_ROW, M // N_ROW), (2 * M) ** -0.5, 0.03125, ((1, 32), (3, 8))),
        "wavelet_inverse": jnp.clip(jax.random.uniform(arg_keys[3], (2,), jnp.float32, 0.3, 0.8), 0.3, 0.8),
    }


def dft_kernel(samples):
    ticks = jnp.arange(samples, dtype=jnp.int32)
    moment = ticks.astype(jnp.float32)
    ramp_len = samples // 8
    rising = 0.5 - 0.5 * jnp.cos(jnp.pi * (moment + 0.5) / ramp_len)
    falling = 0.5 - 0.5 * jnp.cos(jnp.pi * (samples - moment - 0.5) / ramp_len)
    taper = jnp.where(ticks < ramp_len, rising, jnp.where(ticks >= samples - ramp_len, falling, jnp.ones_like(rising)))
    wrapped = ticks * FREQ % samples
    angles = 2.0 * jnp.pi / samples * wrapped.astype(jnp.float32)
    factor = 1.0 / jnp.sqrt(jnp.float32(samples))
    table = jnp.stack([taper * jnp.cos(angles) * factor, -taper * jnp.sin(angles) * factor], axis=1)
    return table.astype(jnp.bfloat16)

def reference(traces, row_source, slice_data, wavelet_inverse):
    kernel = dft_kernel(NT)
    spectra = jnp.dot(traces.reshape(M * PC, NT), kernel, preferred_element_type=jnp.float32).reshape(M, PC, 2)
    spectra = jnp.transpose(spectra, (0, 2, 1)).astype(jnp.bfloat16)
    panel = spectra[row_source]
    real_data = slice_data[0].reshape(M, M)
    imag_data = slice_data[1].reshape(M, M)
    base = panel.astype(jnp.float32)
    wave_real = wavelet_inverse[0]
    wave_imag = wavelet_inverse[1]
    estimate = panel
    pred_real = jnp.zeros((M, PC), jnp.float32)
    pred_imag = jnp.zeros((M, PC), jnp.float32)
    primaries = base
    for iteration in range(ITERS):
        stacked = estimate.reshape(M, 2 * PC)
        real_terms = jnp.dot(real_data, stacked, preferred_element_type=jnp.float32)
        imag_terms = jnp.dot(imag_data, stacked, preferred_element_type=jnp.float32)
        pred_real = real_terms[:, :PC] - imag_terms[:, PC:]
        pred_imag = real_terms[:, PC:] + imag_terms[:, :PC]
        next_real = base[:, 0] - (wave_real * pred_real - wave_imag * pred_imag)
        next_imag = base[:, 1] - (wave_real * pred_imag + wave_imag * pred_real)
        primaries = jnp.stack([next_real, next_imag], axis=1)
        estimate = primaries.astype(jnp.bfloat16)
    multiples = jnp.stack([pred_real, pred_imag], axis=1)
    return (multiples, primaries)
```

```python
import functools

import jax
import jax.numpy as jnp
from jax import lax
from jax.experimental import pallas as pl
from jax.experimental.pallas import tpu as pltpu
from jax.sharding import PartitionSpec as P

FREQ = 61
ITERS = 3
MESH = pl.DeviceIdType.MESH


def dft_kernel(samples):
    ticks = jnp.arange(samples, dtype=jnp.int32)
    moment = ticks.astype(jnp.float32)
    ramp_len = samples // 8
    rising = 0.5 - 0.5 * jnp.cos(jnp.pi * (moment + 0.5) / ramp_len)
    falling = 0.5 - 0.5 * jnp.cos(jnp.pi * (samples - moment - 0.5) / ramp_len)
    taper = jnp.where(
        ticks < ramp_len,
        rising,
        jnp.where(ticks >= samples - ramp_len, falling, jnp.ones_like(rising)),
    )
    wrapped = ticks * FREQ % samples
    angles = 2.0 * jnp.pi / samples * wrapped.astype(jnp.float32)
    factor = 1.0 / jnp.sqrt(jnp.float32(samples))
    table = jnp.stack([taper * jnp.cos(angles) * factor, -taper * jnp.sin(angles) * factor], axis=1)
    return table.astype(jnp.bfloat16)


def predict(n_row, n_zed, rows, lanes, wave_ref, panel_ref, data_ref, mult_ref, prim_ref,
            gathered, matrix, staged, part, mine, swapped, sent, came,
            load_sem, ag_send, ag_recv, sw_send, sw_recv, rs_send, rs_recv):
    row, src = lax.axis_index("row"), lax.axis_index("src")
    zed, core = lax.div(src, 2), lax.rem(src, 2)
    half = lanes // 2
    depth = n_row * rows

    barrier = pltpu.get_barrier_semaphore()

    @pl.loop(1, n_row)
    def _(k):
        pl.semaphore_signal(barrier, inc=1, device_id=(lax.rem(row + k, n_row), src), device_id_type=MESH)

    pl.semaphore_signal(barrier, inc=1, device_id=(row, zed * 2 + 1 - core), device_id_type=MESH)
    for k in range(1, n_zed):
        pl.semaphore_signal(
            barrier, inc=1, device_id=(row, lax.rem(zed + k, n_zed) * 2 + core), device_id_type=MESH
        )
    load = pltpu.make_async_copy(data_ref, staged, load_sem)
    load.start()
    pl.semaphore_wait(barrier, n_row - 1 + 1 + n_zed - 1)

    def send_block(it, k):
        return pltpu.make_async_remote_copy(
            src_ref=gathered.at[it, row],
            dst_ref=gathered.at[it, row],
            send_sem=ag_send.at[it],
            recv_sem=ag_recv.at[it],
            device_id=(lax.rem(row + k, n_row), src),
            device_id_type=MESH,
        )

    def all_but_one(ref):
        return ref.at[pl.ds(0, n_row - 1)]

    gathered[0, row] = panel_ref[...]

    @pl.loop(1, n_row)
    def _(k):
        send_block(0, k).start()

    load.wait()

    @pl.loop(0, 2)
    def _(c):
        @pl.loop(0, depth // 256)
        def _(k):
            at = pl.multiple_of(k * 256, 256)
            turned = staged[c, pl.ds(at, 256), :].T
            for z in range(n_zed):
                matrix[z, c, :, pl.ds(at, 256)] = turned[z * 2 * rows : (z + 1) * 2 * rows, :]

    wave_real, wave_imag = wave_ref[0], wave_ref[1]

    @pl.loop(0, ITERS)
    def _(it):
        pltpu.make_async_copy(all_but_one(gathered.at[it]), all_but_one(gathered.at[it]), ag_recv.at[it]).wait()
        estimate = gathered.at[it].reshape(depth, lanes)

        def swap(step):
            target = lax.rem(zed + step, n_zed)
            return pltpu.make_async_remote_copy(
                src_ref=part.at[it, target, 1 - core],
                dst_ref=swapped.at[it, target],
                send_sem=sw_send.at[it, step],
                recv_sem=sw_recv.at[it, step],
                device_id=(row, zed * 2 + 1 - core),
                device_id_type=MESH,
            )

        def scatter(step):
            target = lax.rem(zed + step, n_zed)
            return pltpu.make_async_remote_copy(
                src_ref=sent.at[it, step],
                dst_ref=came.at[it, step],
                send_sem=rs_send.at[it, step],
                recv_sem=rs_recv.at[it, step],
                device_id=(row, target * 2 + core),
                device_id_type=MESH,
            )

        order = [k for k in (2, 1, 3, 0) if k < n_zed]
        for step in order:
            target = lax.rem(zed + step, n_zed)
            left = matrix.at[target].reshape(2 * 2 * rows, depth)[...]
            terms = jnp.dot(left, estimate[...], preferred_element_type=jnp.float32)
            real_terms, imag_terms = terms[: 2 * rows], terms[2 * rows :]
            real = real_terms[:, :half] - imag_terms[:, half:]
            imag = real_terms[:, half:] + imag_terms[:, :half]
            for c in range(2):
                part[it, target, c, :, :half] = real[c * rows : (c + 1) * rows]
                part[it, target, c, :, half:] = imag[c * rows : (c + 1) * rows]
            swap(step).start()
        for step in order:
            swap(step).wait_recv()
            target = lax.rem(zed + step, n_zed)
            both = part[it, target, core] + swapped[it, target]
            if step:
                sent[it, step] = both.astype(jnp.bfloat16)
                scatter(step).start()
            else:
                mine[...] = both
        total = mine[...]
        for step in order[:-1]:
            scatter(step).wait_recv()
            total = total + came[it, step].astype(jnp.float32)
        real, imag = total[:, :half], total[:, half:]
        base = panel_ref[...].astype(jnp.float32)
        next_real = base[:, :half] - (wave_real * real - wave_imag * imag)
        next_imag = base[:, half:] - (wave_real * imag + wave_imag * real)
        mult_ref[...] = total
        prim_ref[:, :half] = next_real
        prim_ref[:, half:] = next_imag

        @pl.when(it + 1 < ITERS)
        def _():
            gathered[it + 1, row, :, :half] = next_real.astype(jnp.bfloat16)
            gathered[it + 1, row, :, half:] = next_imag.astype(jnp.bfloat16)

            @pl.loop(1, n_row)
            def _(k):
                send_block(it + 1, k).start()

        pltpu.make_async_copy(all_but_one(gathered.at[it]), all_but_one(gathered.at[it]), ag_send.at[it]).wait()
        for step in order:
            swap(step).wait_send()
            if step:
                scatter(step).wait_send()


def body(traces, row_source, slice_data, wavelet_inverse):
    block_rows, shot_local, samples = traces.shape
    n_row, n_src = lax.axis_size("row"), lax.axis_size("src")
    n_zed = n_src // 2
    kernel = dft_kernel(samples)
    spectra = jnp.dot(
        traces.reshape(block_rows * shot_local, samples), kernel, preferred_element_type=jnp.float32
    )
    spectra = jnp.transpose(spectra.reshape(block_rows, shot_local, 2), (0, 2, 1)).astype(
        jnp.bfloat16
    )
    arrived = lax.all_to_all(spectra, "row", split_axis=0, concat_axis=0, tiled=True)
    group_rows = block_rows // n_row
    located = row_source // block_rows * group_rows + row_source % group_rows
    ordered = arrived[located]
    slice_rows = block_rows // n_src
    panel = lax.all_to_all(ordered, "src", split_axis=0, concat_axis=2, tiled=True)
    shot_count = panel.shape[2]
    lanes = 2 * shot_count
    panel = panel.reshape(slice_rows, lanes)
    depth = n_row * slice_rows
    data = jnp.transpose(slice_data, (0, 2, 3, 1)).reshape(2, depth, block_rows)
    f32, bf16 = jnp.float32, jnp.bfloat16
    block = jax.ShapeDtypeStruct((slice_rows, lanes), f32)
    sems = pltpu.SemaphoreType.DMA
    multiples, primaries = pl.pallas_call(
        functools.partial(predict, n_row, n_zed, slice_rows, lanes),
        out_shape=(block, block),
        in_specs=[
            pl.BlockSpec(memory_space=pltpu.SMEM),
            pl.BlockSpec(memory_space=pltpu.VMEM),
            pl.BlockSpec(memory_space=pl.ANY),
        ],
        out_specs=(pl.BlockSpec(memory_space=pltpu.VMEM),) * 2,
        scratch_shapes=[
            pltpu.VMEM((ITERS, n_row, slice_rows, lanes), bf16),
            pltpu.VMEM((n_zed, 2, 2 * slice_rows, depth), bf16),
            pltpu.VMEM((2, depth, block_rows), bf16),
            pltpu.VMEM((ITERS, n_zed, 2, slice_rows, lanes), f32),
            pltpu.VMEM((slice_rows, lanes), f32),
            pltpu.VMEM((ITERS, n_zed, slice_rows, lanes), f32),
            pltpu.VMEM((ITERS, n_zed, slice_rows, lanes), bf16),
            pltpu.VMEM((ITERS, n_zed, slice_rows, lanes), bf16),
            sems,
            sems((ITERS,)),
            sems((ITERS,)),
            sems((ITERS, n_zed)),
            sems((ITERS, n_zed)),
            sems((ITERS, n_zed)),
            sems((ITERS, n_zed)),
        ],
        compiler_params=pltpu.CompilerParams(
            collective_id=0, has_side_effects=True, vmem_limit_bytes=48 << 20
        ),
        name="predict",
    )(wavelet_inverse, panel, data)
    shape = (slice_rows, 2, shot_count)
    return multiples.reshape(shape), primaries.reshape(shape)


def solution(mesh):
    in_specs = (P("row", "src", None), P("row"), P(None, "row", None, "src"), P())
    out_specs = (P(("row", "src"), None, None), P(("row", "src"), None, None))
    return jax.shard_map(body, mesh=mesh, in_specs=in_specs, out_specs=out_specs, check_vma=False)
```

```python
import contextlib
import functools

import jax
import jax.numpy as jnp
from jax import lax
from jax.experimental import pallas as pl
from jax.experimental.pallas import tpu as pltpu
from jax.sharding import PartitionSpec as P

FREQ = 61
ITERS = 3
HALVES = 2
SIDES = (4, 4)
MESH = pl.DeviceIdType.MESH
F32, BF16 = jnp.float32, jnp.bfloat16


def dft_kernel(samples):
    ticks = jnp.arange(samples, dtype=jnp.int32)
    moment = ticks.astype(jnp.float32)
    ramp_len = samples // 8
    rising = 0.5 - 0.5 * jnp.cos(jnp.pi * (moment + 0.5) / ramp_len)
    falling = 0.5 - 0.5 * jnp.cos(jnp.pi * (samples - moment - 0.5) / ramp_len)
    taper = jnp.where(
        ticks < ramp_len,
        rising,
        jnp.where(ticks >= samples - ramp_len, falling, jnp.ones_like(rising)),
    )
    wrapped = ticks * FREQ % samples
    angles = 2.0 * jnp.pi / samples * wrapped.astype(jnp.float32)
    factor = 1.0 / jnp.sqrt(jnp.float32(samples))
    table = (taper * jnp.cos(angles) * factor, -taper * jnp.sin(angles) * factor)
    return [part.astype(BF16).astype(F32).reshape(1, samples) for part in table]


def stage(name):
    return contextlib.nullcontext()


def log2(n):
    assert n & (n - 1) == 0, n
    return n.bit_length() - 1


def iota(shape, axis):
    return lax.broadcasted_iota(jnp.int32, shape, axis)


def predict(
    sizes, wave_ref, real_ref, imag_ref, source_ref, traces_ref, data_ref, mult_ref, prim_ref,
    traces, staged, estimate, spread, place, chosen, spectra, arrived, packed, pieces,
    base, gathered, whole, sent, came,
    tr_sem, load_sem, a_send, a_recv, b_send, b_recv,
    ag_send, ag_recv, ag_beside, rs_send, rs_recv,
):
    n_row, n_src, rows, shot_local, sides = sizes
    n_zed = n_src // 2
    row, src = lax.axis_index("row"), lax.axis_index("src")
    zed, core = lax.div(src, 2), lax.rem(src, 2)
    block_rows = rows * n_src
    group = block_rows // n_row
    depth = n_row * rows
    shots = n_src * shot_local
    per_half = shots // HALVES
    chunks, chunk = traces.shape[0], traces.shape[1]
    packs = rows // group

    def trace_copy(k):
        at = pl.multiple_of(k * chunk, chunk)
        return pltpu.make_async_copy(traces_ref.at[pl.ds(at, chunk)], traces.at[k], tr_sem.at[k])

    ahead = 4
    for k in range(ahead):
        trace_copy(k).start()

    barrier = pltpu.get_barrier_semaphore()

    @pl.loop(1, n_row)
    def _(k):
        pl.semaphore_signal(barrier, inc=1, device_id=(lax.rem(row + k, n_row), src), device_id_type=MESH)

    @pl.loop(1, n_src)
    def _(k):
        pl.semaphore_signal(barrier, inc=1, device_id=(row, lax.rem(src + k, n_src)), device_id_type=MESH)

    load = pltpu.make_async_copy(data_ref, staged, load_sem)

    lanes = 8 * shot_local
    from_lane, to_lane = iota((2 * lanes, lanes), 0), iota((2 * lanes, lanes), 1)
    same = (from_lane >> log2(lanes) == (to_lane >> log2(shot_local) & 1)) & (
        (from_lane ^ to_lane) & (shot_local - 1) == 0
    )
    spread[...] = jnp.where(same, 1.0, 0.0).astype(BF16)
    table_row = iota((16, real_ref.shape[1]), 0)
    table = jnp.where(table_row == 0, real_ref[...], jnp.where(table_row == 1, imag_ref[...], 0.0)).astype(BF16)
    own_lanes = iota((8, lanes), 1) >> log2(shot_local) == iota((8, lanes), 0)

    @pl.loop(0, chunks)
    def _(k):
        with stage("trace wait"):
            trace_copy(k).wait()

        @pl.when(k + ahead < chunks)
        def _():
            trace_copy(k + ahead).start()

        @pl.when(k + ahead == chunks)
        def _():
            load.start()

        spectrum = lax.dot_general(
            table, traces[k], (((1,), (1,)), ((), ())), preferred_element_type=F32
        )
        parts = []
        for c in range(2):
            pieces_of = [
                jnp.where(own_lanes, jnp.broadcast_to(spectrum[c : c + 1, g : g + lanes], (8, lanes)), 0.0)
                for g in range(0, chunk, lanes)
            ]
            parts.append(jnp.concatenate(pieces_of, axis=0).astype(BF16))
        block = jnp.dot(jnp.concatenate(parts, axis=1), spread[...], preferred_element_type=F32)
        block = block.astype(BF16).reshape(-1, group, lanes)
        groups = block.shape[0]
        spectra[pl.ds(k * groups, groups)] = block

    with stage("barrier"):
        pl.semaphore_wait(barrier, n_row - 1 + n_src - 1)

    def to_row(k):
        target = lax.rem(row + k, n_row)
        return pltpu.make_async_remote_copy(
            src_ref=spectra.at[target],
            dst_ref=arrived.at[row],
            send_sem=a_send,
            recv_sem=a_recv,
            device_id=(target, src),
            device_id_type=MESH,
        )

    @pl.loop(1, n_row)
    def _(k):
        to_row(k).start()

    arrived[row] = spectra[row]

    where = source_ref[...]
    located = (where >> log2(block_rows)) * group + (where & (group - 1))
    width = 256
    for at in range(0, block_rows, width):
        hit = iota((block_rows, width), 0) == jnp.broadcast_to(located[:, at : at + width], (block_rows, width))
        turned = jnp.where(hit, 1.0, 0.0).astype(BF16).T
        for u in range(0, width, group):
            device, pack = (at + u) // rows, (at + u) % rows // group
            to = (pack * n_src + device) * group
            chosen[to : to + group, :] = turned[u : u + group, :]

    from_lane, to_lane = iota((n_src * lanes, 2 * shots), 0), iota((n_src * lanes, 2 * shots), 1)
    shot = (from_lane >> log2(lanes)) * shot_local + (from_lane & (shot_local - 1))
    imag = from_lane >> log2(shot_local) & 1
    goal = (shot >> log2(per_half)) * (2 * per_half) + imag * per_half + (shot & (per_half - 1))
    place[...] = jnp.where(goal == to_lane, 1.0, 0.0).astype(BF16)

    def wait_for(ref, count, sem):
        pltpu.make_async_copy(ref.at[pl.ds(0, count)], ref.at[pl.ds(0, count)], sem).wait()

    with stage("row wait"):
        wait_for(arrived, n_row - 1, a_recv)
    ordered = jnp.dot(
        chosen[...], arrived[...].reshape(block_rows, lanes), preferred_element_type=F32
    ).reshape(packs, n_src * group, lanes)
    own_pack = iota((n_src * group, lanes), 1) >> log2(2 * shot_local)
    joined = jnp.zeros((n_src * group, lanes), F32)
    for p in range(packs):
        joined = jnp.where(own_pack == p, ordered[p], joined)
    packed[...] = joined.astype(BF16).reshape(n_src, group, lanes)

    def to_src(k):
        target = lax.rem(src + k, n_src)
        return pltpu.make_async_remote_copy(
            src_ref=packed.at[target],
            dst_ref=pieces.at[src],
            send_sem=b_send,
            recv_sem=b_recv,
            device_id=(row, target),
            device_id_type=MESH,
        )

    @pl.loop(1, n_src)
    def _(k):
        to_src(k).start()

    pieces[src] = packed[src]

    load.wait()

    with stage("src wait"):
        wait_for(pieces, n_src - 1, b_recv)
    lane_pack = iota((group, lanes), 1) >> log2(2 * shot_local)
    left = []
    for s in range(n_src):
        piece = pieces[s].astype(F32)
        left.append(
            jnp.concatenate([jnp.where(lane_pack == p, piece, 0.0) for p in range(packs)], axis=0).astype(BF16)
        )
    panel = jnp.dot(jnp.concatenate(left, axis=1), place[...], preferred_element_type=F32)

    side_x, side_y = sides
    along_x, along_y, along_z = row // (2 * side_y), row // 2 % side_y, row % 2
    beside = row + 1 - 2 * along_z

    def in_plane(k):
        to_x, to_y = lax.rem(along_x + k // side_y, side_x), lax.rem(along_y + k % side_y, side_y)
        return (to_x * side_y + to_y) * 2 + along_z

    def send_block(it, h, slot, target, sem):
        return pltpu.make_async_remote_copy(
            src_ref=gathered.at[it, h, slot],
            dst_ref=gathered.at[it, h, slot],
            send_sem=ag_send.at[it, h],
            recv_sem=sem.at[it, h],
            device_id=(target, src),
            device_id_type=MESH,
        )

    def spread_block(it, h, slot):
        @pl.loop(1, side_x * side_y)
        def _(k):
            send_block(it, h, slot, in_plane(k), ag_recv).start()

    def share(it, h, value):
        gathered[it, h, row] = value.astype(BF16)
        send_block(it, h, row, beside, ag_beside).start()
        spread_block(it, h, row)

    def relay(it, h):
        with stage("relay"):
            send_block(it, h, beside, beside, ag_beside).wait_recv()
        spread_block(it, h, beside)

    width = 2 * per_half
    for h in range(HALVES):
        base[h] = panel[:, h * width : (h + 1) * width]
        share(0, h, base[h])
    for h in range(HALVES):
        relay(0, h)

    def to_owner(it, h, chip, c):
        return pltpu.make_async_remote_copy(
            src_ref=sent.at[it, h, chip, c],
            dst_ref=came.at[it, h, src],
            send_sem=rs_send.at[it, h],
            recv_sem=rs_recv.at[it, h],
            device_id=(row, chip * 2 + c),
            device_id_type=MESH,
        )

    sign = jnp.where(iota((1, width), 1) < per_half, -1.0, 1.0)

    def crossed(v):
        return pltpu.roll(v, per_half, 1) * sign

    def multiply(it, h):
        with stage("gather wait"):
            wait_for(gathered.at[it, h], n_row - 2, ag_recv.at[it, h])
        with stage("multiply"):
            estimate[h] = gathered.at[it, h].reshape(depth, width)[...].T
            for near in range(2):
                pair = lax.rem(zed // 2 + 1 + near, 2)
                columns = pl.ds(pl.multiple_of(pair * 4 * rows, 4 * rows), 4 * rows)
                real_terms, imag_terms = (
                    jnp.dot(estimate[h], staged[c, :, columns], preferred_element_type=F32) for c in range(2)
                )
                real = real_terms[:per_half] - imag_terms[per_half:]
                imag = real_terms[per_half:] + imag_terms[:per_half]
                both = jnp.concatenate([real, imag], axis=0).T.reshape(2, 2, rows, width)
                sent[it, h, pl.ds(pair * 2, 2)] = both.astype(BF16)
                if near:
                    for c in range(2):
                        to_owner(it, h, zed + 1 - 2 * lax.rem(zed, 2), c).start()
                    to_owner(it, h, zed, 1 - core).start()
                    whole[h] = both
                else:
                    for n in range(2):
                        for c in range(2):
                            to_owner(it, h, pair * 2 + n, c).start()

    wave_real, wave_imag = wave_ref[0], wave_ref[1]

    def finish(it, h):
        with stage("sum wait"):
            wait_for(came.at[it, h], n_src - 1, rs_recv.at[it, h])
        total = whole[h, lax.rem(zed, 2), core]
        for k in range(1, n_src):
            total = total + came[it, h, lax.rem(src + k, n_src)].astype(F32)
        return total, base[h] - (wave_real * total + wave_imag * crossed(total))

    @pl.loop(0, ITERS - 1)
    def _(it):
        for h in range(HALVES):
            multiply(it, h)
            if h:
                relay(it + 1, h - 1)
            else:

                @pl.when(it > 0)
                def _():
                    relay(it, HALVES - 1)

            share(it + 1, h, finish(it, h)[1])

    multiply(ITERS - 1, 0)
    relay(ITERS - 1, 1)
    multiply(ITERS - 1, 1)
    for h in range(HALVES):
        total, primary = finish(ITERS - 1, h)
        for c in range(2):
            to = c * shots + h * per_half
            mult_ref[:, to : to + per_half] = total[:, c * per_half : (c + 1) * per_half]
            prim_ref[:, to : to + per_half] = primary[:, c * per_half : (c + 1) * per_half]

    wait_for(spectra, n_row - 1, a_send)
    wait_for(packed, n_src - 1, b_send)

    @pl.loop(0, ITERS)
    def _(it):
        for h in range(HALVES):
            wait_for(gathered.at[it, h], n_row - 1, ag_send.at[it, h])
            wait_for(came.at[it, h], n_src - 1, rs_send.at[it, h])


def body(traces, row_source, slice_data, wavelet_inverse):
    block_rows, shot_local, samples = traces.shape
    n_row, n_src = lax.axis_size("row"), lax.axis_size("src")
    n_zed = n_src // 2
    rows = block_rows // n_src
    group = block_rows // n_row
    shots = n_src * shot_local
    depth = n_row * rows
    width = 2 * shots // HALVES
    lanes = 8 * shot_local
    chunk = 1024
    chunks = block_rows * shot_local // chunk
    real_table, imag_table = dft_kernel(samples)
    data = jnp.transpose(slice_data, (0, 2, 3, 1)).reshape(2, depth, block_rows)
    block = jax.ShapeDtypeStruct((rows, 2 * shots), F32)
    vmem, sems = pltpu.VMEM, pltpu.SemaphoreType.DMA
    multiples, primaries = pl.pallas_call(
        functools.partial(predict, (n_row, n_src, rows, shot_local, SIDES)),
        out_shape=(block, block),
        in_specs=[
            pl.BlockSpec(memory_space=pltpu.SMEM),
            pl.BlockSpec(memory_space=pltpu.VMEM),
            pl.BlockSpec(memory_space=pltpu.VMEM),
            pl.BlockSpec(memory_space=pltpu.VMEM),
            pl.BlockSpec(memory_space=pltpu.HBM),
            pl.BlockSpec(memory_space=pltpu.HBM),
        ],
        out_specs=(pl.BlockSpec(memory_space=pltpu.VMEM),) * 2,
        scratch_shapes=[
            vmem((chunks, chunk, samples), BF16),
            vmem((2, depth, block_rows), BF16),
            vmem((HALVES, width, depth), BF16),
            vmem((2 * lanes, lanes), BF16),
            vmem((n_src * lanes, 2 * shots), BF16),
            vmem((block_rows, block_rows), BF16),
            vmem((n_row, group, lanes), BF16),
            vmem((n_row, group, lanes), BF16),
            vmem((n_src, group, lanes), BF16),
            vmem((n_src, group, lanes), BF16),
            vmem((HALVES, rows, width), F32),
            vmem((ITERS, HALVES, n_row, rows, width), BF16),
            vmem((HALVES, 2, 2, rows, width), F32),
            vmem((ITERS, HALVES, n_zed, 2, rows, width), BF16),
            vmem((ITERS, HALVES, n_src, rows, width), BF16),
            sems((chunks,)),
            sems,
            sems,
            sems,
            sems,
            sems,
            sems((ITERS, HALVES)),
            sems((ITERS, HALVES)),
            sems((ITERS, HALVES)),
            sems((ITERS, HALVES)),
            sems((ITERS, HALVES)),
        ],
        compiler_params=pltpu.CompilerParams(
            collective_id=0, has_side_effects=True, vmem_limit_bytes=52 << 20
        ),
        name="predict",
    )(
        wavelet_inverse,
        real_table,
        imag_table,
        row_source.reshape(1, block_rows),
        traces.reshape(block_rows * shot_local, samples),
        data,
    )
    shape = (rows, 2, shots)
    return multiples.reshape(shape), primaries.reshape(shape)


def solution(mesh):
    in_specs = (P("row", "src", None), P("row"), P(None, "row", None, "src"), P())
    out_specs = (P(("row", "src"), None, None), P(("row", "src"), None, None))
    return jax.shard_map(body, mesh=mesh, in_specs=in_specs, out_specs=out_specs, check_vma=False)
```

```python
import contextlib
import functools

import jax
import jax.numpy as jnp
from jax import lax
from jax.experimental import pallas as pl
from jax.experimental.pallas import tpu as pltpu
from jax.sharding import PartitionSpec as P

FREQ = 61
ITERS = 3
HALVES = 2
NEAR = 4
SIDES = (4, 4)
MESH = pl.DeviceIdType.MESH
F32, BF16 = jnp.float32, jnp.bfloat16


def dft_kernel(samples, lines):
    ticks, line = iota((lines, samples), 1), iota((lines, samples), 0)
    moment = ticks.astype(jnp.float32)
    ramp_len = samples // 8
    rising = 0.5 - 0.5 * jnp.cos(jnp.pi * (moment + 0.5) / ramp_len)
    falling = 0.5 - 0.5 * jnp.cos(jnp.pi * (samples - moment - 0.5) / ramp_len)
    taper = jnp.where(
        ticks < ramp_len,
        rising,
        jnp.where(ticks >= samples - ramp_len, falling, jnp.ones_like(rising)),
    )
    wrapped = ticks * FREQ % samples
    angles = 2.0 * jnp.pi / samples * wrapped.astype(jnp.float32)
    factor = 1.0 / jnp.sqrt(jnp.float32(samples))
    table = jnp.where(line == 0, taper * jnp.cos(angles) * factor, -taper * jnp.sin(angles) * factor)
    return table.astype(BF16).astype(F32)


def stage(name):
    return contextlib.nullcontext()


def log2(n):
    assert n & (n - 1) == 0, n
    return n.bit_length() - 1


def iota(shape, axis):
    return lax.broadcasted_iota(jnp.int32, shape, axis)


def predict(
    sizes, small_ref, traces_ref, data_ref, mult_ref, prim_ref,
    traces, staged, estimate, first, spread, place, chosen, spectra, arrived, packed, pieces,
    base, gathered, whole, sent, came,
    tr_sem, load_sem, a_send, a_recv, b_send, b_recv,
    ag_send, ag_recv, ag_other, ag_beside, rs_send, rs_recv,
):
    n_row, n_src, rows, shot_local, sides = sizes
    n_zed = n_src // 2
    row, src = lax.axis_index("row"), lax.axis_index("src")
    zed, core = lax.div(src, 2), lax.rem(src, 2)
    block_rows = rows * n_src
    group = block_rows // n_row
    depth = n_row * rows
    shots = n_src * shot_local
    per_half = shots // HALVES
    chunks, chunk = traces.shape[0], traces.shape[1]
    packs = rows // group

    def trace_copy(k):
        return pltpu.make_async_copy(traces_ref.at[pl.ds(k * chunk, chunk)], traces.at[k], tr_sem.at[k])

    ahead = 4
    for k in range(ahead):
        trace_copy(k).start()

    barrier = pltpu.get_barrier_semaphore()

    @pl.loop(1, n_row)
    def _(k):
        pl.semaphore_signal(barrier, inc=1, device_id=(lax.rem(row + k, n_row), src), device_id_type=MESH)

    @pl.loop(1, n_src)
    def _(k):
        pl.semaphore_signal(barrier, inc=1, device_id=(row, lax.rem(src + k, n_src)), device_id_type=MESH)

    loads = [
        pltpu.make_async_copy(data_ref.at[c, :, z], staged.at[c, z], load_sem.at[c, z]) for c in range(2) for z in range(2)
    ]

    lanes = 8 * shot_local
    from_lane, to_lane = iota((2 * lanes, lanes), 0), iota((2 * lanes, lanes), 1)
    same = (from_lane >> log2(lanes) == (to_lane >> log2(shot_local) & 1)) & (
        (from_lane ^ to_lane) & (shot_local - 1) == 0
    )
    spread[...] = jnp.where(same, 1.0, 0.0).astype(BF16)
    samples = small_ref.shape[1]
    table_row = iota((16, samples), 0)
    table = jnp.where(table_row == 0, small_ref[0:1], jnp.where(table_row == 1, small_ref[1:2], 0.0)).astype(BF16)
    own_lanes = iota((8, lanes), 1) >> log2(shot_local) == iota((8, lanes), 0)

    for k in range(chunks):
        with stage("trace wait"):
            trace_copy(k).wait()

        if k + ahead < chunks:
            trace_copy(k + ahead).start()
        if k + ahead == chunks:
            for load in loads:
                load.start()

        spectrum = lax.dot_general(
            table, traces[k], (((1,), (1,)), ((), ())), preferred_element_type=F32
        )
        parts = []
        for c in range(2):
            pieces_of = [
                jnp.where(own_lanes, jnp.broadcast_to(spectrum[c : c + 1, g : g + lanes], (8, lanes)), 0.0)
                for g in range(0, chunk, lanes)
            ]
            parts.append(jnp.concatenate(pieces_of, axis=0).astype(BF16))
        block = jnp.dot(jnp.concatenate(parts, axis=1), spread[...], preferred_element_type=F32)
        block = block.astype(BF16).reshape(-1, group, lanes)
        groups = block.shape[0]
        spectra[k * groups : (k + 1) * groups] = block

    with stage("barrier"):
        pl.semaphore_wait(barrier, n_row - 1 + n_src - 1)

    def to_row(k):
        target = lax.rem(row + k, n_row)
        return pltpu.make_async_remote_copy(
            src_ref=spectra.at[target],
            dst_ref=arrived.at[row],
            send_sem=a_send,
            recv_sem=a_recv,
            device_id=(target, src),
            device_id_type=MESH,
        )

    @pl.loop(1, n_row)
    def _(k):
        to_row(k).start()

    arrived[row] = spectra[row]

    where = small_ref[2:3].astype(jnp.int32)
    located = (where >> log2(block_rows)) * group + (where & (group - 1))
    width = 256
    for at in range(0, block_rows, width):
        hit = iota((block_rows, width), 0) == jnp.broadcast_to(located[:, at : at + width], (block_rows, width))
        turned = jnp.where(hit, 1.0, 0.0).astype(BF16).T
        for u in range(0, width, group):
            device, pack = (at + u) // rows, (at + u) % rows // group
            to = (pack * n_src + device) * group
            chosen[to : to + group, :] = turned[u : u + group, :]

    from_lane, to_lane = iota((n_src * lanes, 2 * shots), 0), iota((n_src * lanes, 2 * shots), 1)
    shot = (from_lane >> log2(lanes)) * shot_local + (from_lane & (shot_local - 1))
    imag = from_lane >> log2(shot_local) & 1
    goal = (shot >> log2(per_half)) * (2 * per_half) + imag * per_half + (shot & (per_half - 1))
    place[...] = jnp.where(goal == to_lane, 1.0, 0.0).astype(BF16)

    def wait_for(ref, count, sem):
        pltpu.make_async_copy(ref.at[pl.ds(0, count)], ref.at[pl.ds(0, count)], sem).wait()

    with stage("row wait"):
        wait_for(arrived, n_row - 1, a_recv)
    ordered = jnp.dot(
        chosen[...], arrived[...].reshape(block_rows, lanes), preferred_element_type=F32
    ).reshape(packs, n_src * group, lanes)
    own_pack = iota((n_src * group, lanes), 1) >> log2(2 * shot_local)
    joined = jnp.zeros((n_src * group, lanes), F32)
    for p in range(packs):
        joined = jnp.where(own_pack == p, ordered[p], joined)
    packed[...] = joined.astype(BF16).reshape(n_src, group, lanes)

    def to_src(k):
        target = lax.rem(src + k, n_src)
        return pltpu.make_async_remote_copy(
            src_ref=packed.at[target],
            dst_ref=pieces.at[src],
            send_sem=b_send,
            recv_sem=b_recv,
            device_id=(row, target),
            device_id_type=MESH,
        )

    @pl.loop(1, n_src)
    def _(k):
        to_src(k).start()

    pieces[src] = packed[src]

    for load in loads:
        load.wait()

    with stage("src wait"):
        wait_for(pieces, n_src - 1, b_recv)
    lane_pack = iota((group, lanes), 1) >> log2(2 * shot_local)
    left = []
    for s in range(n_src):
        piece = pieces[s].astype(F32)
        left.append(
            jnp.concatenate([jnp.where(lane_pack == p, piece, 0.0) for p in range(packs)], axis=0).astype(BF16)
        )
    panel = jnp.dot(jnp.concatenate(left, axis=1), place[...], preferred_element_type=F32)

    side_x, side_y = sides
    along_x, along_y, along_z = row // (2 * side_y), row // 2 % side_y, row % 2
    plane = side_x * side_y
    beside = row + 1 - 2 * along_z
    other_z = 1 - along_z
    slot = along_z * plane + row // 2
    slot_beside = other_z * plane + row // 2

    def away(x, y):
        return min(x, side_x - x) + min(y, side_y - y)

    offsets = [(x, y) for x in range(side_x) for y in range(side_y) if x or y]
    offsets.sort(key=lambda o: -away(*o))
    far = [o for o in offsets if away(*o) > NEAR]
    near = [o for o in offsets if away(*o) <= NEAR]

    def send_block(it, h, which, target, sem):
        return pltpu.make_async_remote_copy(
            src_ref=gathered.at[it, h, which],
            dst_ref=gathered.at[it, h, which],
            send_sem=ag_send.at[it, h],
            recv_sem=sem.at[it, h],
            device_id=(target, src),
            device_id_type=MESH,
        )

    def send_over(it, h, which, chips, to_z, sem):
        for x, y in chips:
            to_x, to_y = lax.rem(along_x + x, side_x), lax.rem(along_y + y, side_y)
            send_block(it, h, which, (to_x * side_y + to_y) * 2 + to_z, sem).start()

    def share(it, h, value):
        gathered[it, h, slot] = value.astype(BF16)
        send_block(it, h, slot, beside, ag_beside).start()
        send_over(it, h, slot, far, other_z, ag_other)
        send_over(it, h, slot, offsets, along_z, ag_recv)

    def relay(it, h):
        with stage("relay"):
            send_block(it, h, slot_beside, beside, ag_beside).wait_recv()
        send_over(it, h, slot_beside, near, along_z, ag_other)

    width = 2 * per_half
    for h in range(HALVES):
        base[h] = panel[:, h * width : (h + 1) * width]
        share(0, h, base[h])
        if h == 0:
            relay(0, 0)

    def to_owner(it, h, chip, c):
        return pltpu.make_async_remote_copy(
            src_ref=sent.at[it, h, chip, c],
            dst_ref=came.at[it, h, src],
            send_sem=rs_send.at[it, h],
            recv_sem=rs_recv.at[it, h],
            device_id=(row, chip * 2 + c),
            device_id_type=MESH,
        )

    sign = jnp.where(iota((1, width), 1) < per_half, -1.0, 1.0)

    def crossed(v):
        return pltpu.roll(v, per_half, 1) * sign

    def multiply(it, h):
        def terms_of(z, pair):
            columns = pl.ds(pl.multiple_of(pair * 4 * rows, 4 * rows), 4 * rows)
            real_terms, imag_terms = (
                jnp.dot(
                    estimate[h],
                    staged.at[c, z].reshape(depth // 2, block_rows)[:, columns],
                    preferred_element_type=F32,
                )
                for c in range(2)
            )
            real = real_terms[:per_half] - imag_terms[per_half:]
            imag = real_terms[per_half:] + imag_terms[:per_half]
            return jnp.concatenate([real, imag], axis=0)

        def turn(z):
            at = pl.multiple_of(z * plane, plane)
            estimate[h] = gathered.at[it, h, pl.ds(at, plane)].reshape(depth // 2, width)[...].T

        pairs = [lax.rem(zed // 2 + 1 + n, 2) for n in range(2)]
        with stage("plane wait"):
            wait_for(gathered.at[it, h], plane - 1, ag_recv.at[it, h])
        with stage("multiply plane"):
            turn(along_z)
            for n in range(2):
                first[n] = terms_of(along_z, pairs[n])
        with stage("gather wait"):
            wait_for(gathered.at[it, h], plane - 1, ag_other.at[it, h])
        with stage("multiply"):
            turn(other_z)
            for n, pair in enumerate(pairs):
                both = first[n] + terms_of(other_z, pair)
                sent[it, h, pl.ds(pair * 2, 2)] = both.astype(BF16).T.reshape(2, 2, rows, width)
                if n:
                    for c in range(2):
                        to_owner(it, h, zed + 1 - 2 * lax.rem(zed, 2), c).start()
                    to_owner(it, h, zed, 1 - core).start()
                    whole[h] = both.T.reshape(2, 2, rows, width)
                else:
                    for chip in range(2):
                        for c in range(2):
                            to_owner(it, h, pair * 2 + lax.rem(zed + chip, 2), c).start()

    wave_real, wave_imag = small_ref[3:4, :width], small_ref[4:5, :width]

    def finish(it, h):
        with stage("sum wait"):
            wait_for(came.at[it, h], n_src - 1, rs_recv.at[it, h])
        total = whole[h, lax.rem(zed, 2), core]
        for k in range(1, n_src):
            total = total + came[it, h, lax.rem(src + k, n_src)].astype(F32)
        return total, base[h] - (wave_real * total + wave_imag * crossed(total))

    @pl.loop(0, ITERS - 1)
    def _(it):
        for h in range(HALVES):
            multiply(it, h)
            relay(it + h, 1 - h)
            share(it + 1, h, finish(it, h)[1])

    multiply(ITERS - 1, 0)
    relay(ITERS - 1, 1)
    multiply(ITERS - 1, 1)
    for h in range(HALVES):
        total, primary = finish(ITERS - 1, h)
        for c in range(2):
            to = c * shots + h * per_half
            mult_ref[:, to : to + per_half] = total[:, c * per_half : (c + 1) * per_half]
            prim_ref[:, to : to + per_half] = primary[:, c * per_half : (c + 1) * per_half]

    wait_for(spectra, n_row - 1, a_send)
    wait_for(packed, n_src - 1, b_send)

    @pl.loop(0, ITERS)
    def _(it):
        for h in range(HALVES):
            wait_for(gathered.at[it, h], n_row - 1, ag_send.at[it, h])
            wait_for(came.at[it, h], n_src - 1, rs_send.at[it, h])


def body(traces, row_source, slice_data, wavelet_inverse):
    block_rows, shot_local, samples = traces.shape
    n_row, n_src = lax.axis_size("row"), lax.axis_size("src")
    n_zed = n_src // 2
    rows = block_rows // n_src
    group = block_rows // n_row
    shots = n_src * shot_local
    depth = n_row * rows
    width = 2 * shots // HALVES
    lanes = 8 * shot_local
    chunk = 1024
    chunks = block_rows * shot_local // chunk
    lines = 8
    line = iota((lines, samples), 0)
    wave = lax.broadcast_in_dim(jnp.pad(wavelet_inverse, (3, lines - 5)), (lines, samples), (0,))
    source = lax.broadcast_in_dim(row_source.astype(F32), (lines, samples), (1,))
    small = jnp.where(line == 2, source, jnp.where(line > 2, wave, dft_kernel(samples, lines)))
    data = jnp.transpose(slice_data, (0, 2, 3, 1)).reshape(2, n_row // 2, 2, rows, block_rows)
    block = jax.ShapeDtypeStruct((rows, 2 * shots), F32)
    vmem, sems = pltpu.VMEM, pltpu.SemaphoreType.DMA
    multiples, primaries = pl.pallas_call(
        functools.partial(predict, (n_row, n_src, rows, shot_local, SIDES)),
        out_shape=(block, block),
        in_specs=[
            pl.BlockSpec(memory_space=pltpu.VMEM),
            pl.BlockSpec(memory_space=pltpu.HBM),
            pl.BlockSpec(memory_space=pltpu.HBM),
        ],
        out_specs=(pl.BlockSpec(memory_space=pltpu.VMEM),) * 2,
        scratch_shapes=[
            vmem((chunks, chunk, samples), BF16),
            vmem((2, 2, n_row // 2, rows, block_rows), BF16),
            vmem((HALVES, width, depth // 2), BF16),
            vmem((2, width, 4 * rows), F32),
            vmem((2 * lanes, lanes), BF16),
            vmem((n_src * lanes, 2 * shots), BF16),
            vmem((block_rows, block_rows), BF16),
            vmem((n_row, group, lanes), BF16),
            vmem((n_row, group, lanes), BF16),
            vmem((n_src, group, lanes), BF16),
            vmem((n_src, group, lanes), BF16),
            vmem((HALVES, rows, width), F32),
            vmem((ITERS, HALVES, n_row, rows, width), BF16),
            vmem((HALVES, 2, 2, rows, width), F32),
            vmem((ITERS, HALVES, n_zed, 2, rows, width), BF16),
            vmem((ITERS, HALVES, n_src, rows, width), BF16),
            sems((chunks,)),
            sems((2, 2)),
            sems,
            sems,
            sems,
            sems,
            sems((ITERS, HALVES)),
            sems((ITERS, HALVES)),
            sems((ITERS, HALVES)),
            sems((ITERS, HALVES)),
            sems((ITERS, HALVES)),
            sems((ITERS, HALVES)),
        ],
        compiler_params=pltpu.CompilerParams(
            collective_id=0, has_side_effects=True, vmem_limit_bytes=52 << 20
        ),
        name="predict",
    )(
        small,
        traces.reshape(block_rows * shot_local, samples),
        data,
    )
    shape = (rows, 2, shots)
    return multiples.reshape(shape), primaries.reshape(shape)


def solution(mesh):
    in_specs = (P("row", "src", None), P("row"), P(None, "row", None, "src"), P())
    out_specs = (P(("row", "src"), None, None), P(("row", "src"), None, None))
    return jax.shard_map(body, mesh=mesh, in_specs=in_specs, out_specs=out_specs, check_vma=False)
```

```python
import contextlib
import functools

import jax
import jax.numpy as jnp
from jax import lax
from jax.experimental import pallas as pl
from jax.experimental.pallas import tpu as pltpu
from jax.sharding import PartitionSpec as P

FREQ = 61
ITERS = 3
HALVES = 2
NEAR = 4
SIDES = (4, 4)
MESH = pl.DeviceIdType.MESH
F32, BF16 = jnp.float32, jnp.bfloat16


def dft_kernel(samples, lines):
    ticks, line = iota((lines, samples), 1), iota((lines, samples), 0)
    moment = ticks.astype(jnp.float32)
    ramp_len = samples // 8
    rising = 0.5 - 0.5 * jnp.cos(jnp.pi * (moment + 0.5) / ramp_len)
    falling = 0.5 - 0.5 * jnp.cos(jnp.pi * (samples - moment - 0.5) / ramp_len)
    taper = jnp.where(
        ticks < ramp_len,
        rising,
        jnp.where(ticks >= samples - ramp_len, falling, jnp.ones_like(rising)),
    )
    wrapped = ticks * FREQ % samples
    angles = 2.0 * jnp.pi / samples * wrapped.astype(jnp.float32)
    factor = 1.0 / jnp.sqrt(jnp.float32(samples))
    table = jnp.where(line == 0, taper * jnp.cos(angles) * factor, -taper * jnp.sin(angles) * factor)
    return table.astype(BF16).astype(F32)


def stage(name):
    return contextlib.nullcontext()


def log2(n):
    assert n & (n - 1) == 0, n
    return n.bit_length() - 1


def iota(shape, axis):
    return lax.broadcasted_iota(jnp.int32, shape, axis)


def predict(
    sizes, table_ref, small_ref, traces_ref, data_ref, mult_ref, prim_ref,
    traces, staged, estimate, first, spread, place, chosen, spectra, arrived, packed, pieces,
    base, gathered, whole, sent, came,
    tr_sem, load_sem, a_send, a_recv, b_send, b_recv,
    ag_send, ag_recv, ag_other, ag_beside, rs_send, rs_recv,
):
    n_row, n_src, rows, shot_local, sides = sizes
    n_zed = n_src // 2
    row, src = lax.axis_index("row"), lax.axis_index("src")
    zed, core = lax.div(src, 2), lax.rem(src, 2)
    block_rows = rows * n_src
    group = block_rows // n_row
    depth = n_row * rows
    shots = n_src * shot_local
    per_half = shots // HALVES
    chunks, chunk = traces.shape[0], traces.shape[1]
    packs = rows // group

    def trace_copy(k):
        return pltpu.make_async_copy(traces_ref.at[pl.ds(k * chunk, chunk)], traces.at[k], tr_sem.at[k])

    ahead = 4
    for k in range(ahead):
        trace_copy(k).start()

    barrier = pltpu.get_barrier_semaphore()

    @pl.loop(1, n_row)
    def _(k):
        pl.semaphore_signal(barrier, inc=1, device_id=(lax.rem(row + k, n_row), src), device_id_type=MESH)

    @pl.loop(1, n_src)
    def _(k):
        pl.semaphore_signal(barrier, inc=1, device_id=(row, lax.rem(src + k, n_src)), device_id_type=MESH)

    loads = [
        pltpu.make_async_copy(data_ref.at[c, :, z], staged.at[c, z], load_sem.at[c, z]) for c in range(2) for z in range(2)
    ]

    lanes = 8 * shot_local
    from_lane, to_lane = iota((2 * lanes, lanes), 0), iota((2 * lanes, lanes), 1)
    same = (from_lane >> log2(lanes) == (to_lane >> log2(shot_local) & 1)) & (
        (from_lane ^ to_lane) & (shot_local - 1) == 0
    )
    spread[...] = jnp.where(same, 1.0, 0.0).astype(BF16)
    samples = table_ref.shape[1]
    table_row = iota((16, samples), 0)
    table = jnp.where(table_row == 0, table_ref[0:1], jnp.where(table_row == 1, table_ref[1:2], 0.0)).astype(BF16)
    own_lanes = iota((8, lanes), 1) >> log2(shot_local) == iota((8, lanes), 0)

    for k in range(chunks):
        with stage("trace wait"):
            trace_copy(k).wait()

        if k + ahead < chunks:
            trace_copy(k + ahead).start()
        if k + ahead == chunks:
            for load in loads:
                load.start()

        spectrum = lax.dot_general(
            table, traces[k], (((1,), (1,)), ((), ())), preferred_element_type=F32
        )
        parts = []
        for c in range(2):
            pieces_of = [
                jnp.where(own_lanes, jnp.broadcast_to(spectrum[c : c + 1, g : g + lanes], (8, lanes)), 0.0)
                for g in range(0, chunk, lanes)
            ]
            parts.append(jnp.concatenate(pieces_of, axis=0).astype(BF16))
        block = jnp.dot(jnp.concatenate(parts, axis=1), spread[...], preferred_element_type=F32)
        block = block.astype(BF16).reshape(-1, group, lanes)
        groups = block.shape[0]
        spectra[k * groups : (k + 1) * groups] = block

    with stage("barrier"):
        pl.semaphore_wait(barrier, n_row - 1 + n_src - 1)

    def to_row(k):
        target = lax.rem(row + k, n_row)
        return pltpu.make_async_remote_copy(
            src_ref=spectra.at[target],
            dst_ref=arrived.at[row],
            send_sem=a_send,
            recv_sem=a_recv,
            device_id=(target, src),
            device_id_type=MESH,
        )

    @pl.loop(1, n_row)
    def _(k):
        to_row(k).start()

    arrived[row] = spectra[row]

    where = small_ref[:, :block_rows].astype(jnp.int32)
    located = (where >> log2(block_rows)) * group + (where & (group - 1))
    width = 256
    for at in range(0, block_rows, width):
        hit = iota((block_rows, width), 0) == jnp.broadcast_to(located[:, at : at + width], (block_rows, width))
        turned = jnp.where(hit, 1.0, 0.0).astype(BF16).T
        for u in range(0, width, group):
            device, pack = (at + u) // rows, (at + u) % rows // group
            to = (pack * n_src + device) * group
            chosen[to : to + group, :] = turned[u : u + group, :]

    from_lane, to_lane = iota((n_src * lanes, 2 * shots), 0), iota((n_src * lanes, 2 * shots), 1)
    shot = (from_lane >> log2(lanes)) * shot_local + (from_lane & (shot_local - 1))
    imag = from_lane >> log2(shot_local) & 1
    goal = (shot >> log2(per_half)) * (2 * per_half) + imag * per_half + (shot & (per_half - 1))
    place[...] = jnp.where(goal == to_lane, 1.0, 0.0).astype(BF16)

    def wait_for(ref, count, sem):
        pltpu.make_async_copy(ref.at[pl.ds(0, count)], ref.at[pl.ds(0, count)], sem).wait()

    with stage("row wait"):
        wait_for(arrived, n_row - 1, a_recv)
    ordered = jnp.dot(
        chosen[...], arrived[...].reshape(block_rows, lanes), preferred_element_type=F32
    ).reshape(packs, n_src * group, lanes)
    own_pack = iota((n_src * group, lanes), 1) >> log2(2 * shot_local)
    joined = jnp.zeros((n_src * group, lanes), F32)
    for p in range(packs):
        joined = jnp.where(own_pack == p, ordered[p], joined)
    packed[...] = joined.astype(BF16).reshape(n_src, group, lanes)

    def to_src(k):
        target = lax.rem(src + k, n_src)
        return pltpu.make_async_remote_copy(
            src_ref=packed.at[target],
            dst_ref=pieces.at[src],
            send_sem=b_send,
            recv_sem=b_recv,
            device_id=(row, target),
            device_id_type=MESH,
        )

    @pl.loop(1, n_src)
    def _(k):
        to_src(k).start()

    pieces[src] = packed[src]

    for load in loads:
        load.wait()

    with stage("src wait"):
        wait_for(pieces, n_src - 1, b_recv)
    lane_pack = iota((group, lanes), 1) >> log2(2 * shot_local)
    left = []
    for s in range(n_src):
        piece = pieces[s].astype(F32)
        left.append(
            jnp.concatenate([jnp.where(lane_pack == p, piece, 0.0) for p in range(packs)], axis=0).astype(BF16)
        )
    panel = jnp.dot(jnp.concatenate(left, axis=1), place[...], preferred_element_type=F32)

    side_x, side_y = sides
    along_x, along_y, along_z = row // (2 * side_y), row // 2 % side_y, row % 2
    plane = side_x * side_y
    beside = row + 1 - 2 * along_z
    other_z = 1 - along_z
    slot = along_z * plane + row // 2
    slot_beside = other_z * plane + row // 2

    def away(x, y):
        return min(x, side_x - x) + min(y, side_y - y)

    offsets = [(x, y) for x in range(side_x) for y in range(side_y) if x or y]
    offsets.sort(key=lambda o: -away(*o))
    far = [o for o in offsets if away(*o) > NEAR]
    near = [o for o in offsets if away(*o) <= NEAR]

    def send_block(it, h, which, target, sem):
        return pltpu.make_async_remote_copy(
            src_ref=gathered.at[it, h, which],
            dst_ref=gathered.at[it, h, which],
            send_sem=ag_send.at[it, h],
            recv_sem=sem.at[it, h],
            device_id=(target, src),
            device_id_type=MESH,
        )

    def send_over(it, h, which, chips, to_z, sem):
        for x, y in chips:
            to_x = lax.rem(along_x + side_x + x - 2 * core * x + core * side_x, side_x)
            to_y = lax.rem(along_y + side_y + y - 2 * core * y + core * side_y, side_y)
            send_block(it, h, which, (to_x * side_y + to_y) * 2 + to_z, sem).start()

    def share(it, h, value):
        gathered[it, h, slot] = value.astype(BF16)
        send_block(it, h, slot, beside, ag_beside).start()
        send_over(it, h, slot, far, other_z, ag_other)
        send_over(it, h, slot, offsets, along_z, ag_recv)

    def relay(it, h):
        with stage("relay"):
            send_block(it, h, slot_beside, beside, ag_beside).wait_recv()
        send_over(it, h, slot_beside, near, along_z, ag_other)

    width = 2 * per_half
    for h in range(HALVES):
        base[h] = panel[:, h * width : (h + 1) * width]
        share(0, h, base[h])
        if h == 0:
            relay(0, 0)

    def to_owner(it, h, chip, c):
        return pltpu.make_async_remote_copy(
            src_ref=sent.at[it, h, chip, c],
            dst_ref=came.at[it, h, src],
            send_sem=rs_send.at[it, h],
            recv_sem=rs_recv.at[it, h],
            device_id=(row, chip * 2 + c),
            device_id_type=MESH,
        )

    sign = jnp.where(iota((1, width), 1) < per_half, -1.0, 1.0)

    def crossed(v):
        return pltpu.roll(v, per_half, 1) * sign

    def multiply(it, h):
        def terms_of(z, pair):
            columns = pl.ds(pl.multiple_of(pair * 4 * rows, 4 * rows), 4 * rows)
            real_terms, imag_terms = (
                jnp.dot(
                    estimate[h],
                    staged.at[c, z].reshape(depth // 2, block_rows)[:, columns],
                    preferred_element_type=F32,
                )
                for c in range(2)
            )
            real = real_terms[:per_half] - imag_terms[per_half:]
            imag = real_terms[per_half:] + imag_terms[:per_half]
            return jnp.concatenate([real, imag], axis=0)

        def turn(z):
            at = pl.multiple_of(z * plane, plane)
            estimate[h] = gathered.at[it, h, pl.ds(at, plane)].reshape(depth // 2, width)[...].T

        pairs = [lax.rem(zed // 2 + 1 + n, 2) for n in range(2)]
        with stage("plane wait"):
            wait_for(gathered.at[it, h], plane - 1, ag_recv.at[it, h])
        with stage("multiply plane"):
            turn(along_z)
            for n in range(2):
                first[n] = terms_of(along_z, pairs[n])
        with stage("gather wait"):
            wait_for(gathered.at[it, h], plane - 1, ag_other.at[it, h])
        with stage("multiply"):
            turn(other_z)
            for n, pair in enumerate(pairs):
                both = first[n] + terms_of(other_z, pair)
                sent[it, h, pl.ds(pair * 2, 2)] = both.astype(BF16).T.reshape(2, 2, rows, width)
                if n:
                    for c in range(2):
                        to_owner(it, h, zed + 1 - 2 * lax.rem(zed, 2), c).start()
                    to_owner(it, h, zed, 1 - core).start()
                    whole[h] = both.T.reshape(2, 2, rows, width)
                else:
                    for chip in range(2):
                        for c in range(2):
                            to_owner(it, h, pair * 2 + lax.rem(zed + chip, 2), c).start()

    wave_real, wave_imag = small_ref[:, block_rows : block_rows + 1], small_ref[:, block_rows + 1 : block_rows + 2]

    def finish(it, h):
        with stage("sum wait"):
            wait_for(came.at[it, h], n_src - 1, rs_recv.at[it, h])
        total = whole[h, lax.rem(zed, 2), core]
        for k in range(1, n_src):
            total = total + came[it, h, lax.rem(src + k, n_src)].astype(F32)
        return total, base[h] - (wave_real * total + wave_imag * crossed(total))

    @pl.loop(0, ITERS - 1)
    def _(it):
        for h in range(HALVES):
            multiply(it, h)
            relay(it + h, 1 - h)
            share(it + 1, h, finish(it, h)[1])

    multiply(ITERS - 1, 0)
    relay(ITERS - 1, 1)
    multiply(ITERS - 1, 1)
    for h in range(HALVES):
        total, primary = finish(ITERS - 1, h)
        for c in range(2):
            to = c * shots + h * per_half
            mult_ref[:, to : to + per_half] = total[:, c * per_half : (c + 1) * per_half]
            prim_ref[:, to : to + per_half] = primary[:, c * per_half : (c + 1) * per_half]

    wait_for(spectra, n_row - 1, a_send)
    wait_for(packed, n_src - 1, b_send)

    @pl.loop(0, ITERS)
    def _(it):
        for h in range(HALVES):
            wait_for(gathered.at[it, h], n_row - 1, ag_send.at[it, h])
            wait_for(came.at[it, h], n_src - 1, rs_send.at[it, h])


def body(traces, row_source, slice_data, wavelet_inverse):
    block_rows, shot_local, samples = traces.shape
    n_row, n_src = lax.axis_size("row"), lax.axis_size("src")
    n_zed = n_src // 2
    rows = block_rows // n_src
    group = block_rows // n_row
    shots = n_src * shot_local
    depth = n_row * rows
    width = 2 * shots // HALVES
    lanes = 8 * shot_local
    chunk = 1024
    chunks = block_rows * shot_local // chunk
    lines = 8
    small = jnp.pad(row_source, (0, 128)).astype(F32) + jnp.pad(wavelet_inverse, (block_rows, 126))
    small = small.reshape(1, -1)
    table = dft_kernel(samples, lines)
    data = jnp.transpose(slice_data, (0, 2, 3, 1)).reshape(2, n_row // 2, 2, rows, block_rows)
    block = jax.ShapeDtypeStruct((rows, 2 * shots), F32)
    vmem, sems = pltpu.VMEM, pltpu.SemaphoreType.DMA
    multiples, primaries = pl.pallas_call(
        functools.partial(predict, (n_row, n_src, rows, shot_local, SIDES)),
        out_shape=(block, block),
        in_specs=[
            pl.BlockSpec(memory_space=pltpu.VMEM),
            pl.BlockSpec(memory_space=pltpu.VMEM),
            pl.BlockSpec(memory_space=pltpu.HBM),
            pl.BlockSpec(memory_space=pltpu.HBM),
        ],
        out_specs=(pl.BlockSpec(memory_space=pltpu.VMEM),) * 2,
        scratch_shapes=[
            vmem((chunks, chunk, samples), BF16),
            vmem((2, 2, n_row // 2, rows, block_rows), BF16),
            vmem((HALVES, width, depth // 2), BF16),
            vmem((2, width, 4 * rows), F32),
            vmem((2 * lanes, lanes), BF16),
            vmem((n_src * lanes, 2 * shots), BF16),
            vmem((block_rows, block_rows), BF16),
            vmem((n_row, group, lanes), BF16),
            vmem((n_row, group, lanes), BF16),
            vmem((n_src, group, lanes), BF16),
            vmem((n_src, group, lanes), BF16),
            vmem((HALVES, rows, width), F32),
            vmem((ITERS, HALVES, n_row, rows, width), BF16),
            vmem((HALVES, 2, 2, rows, width), F32),
            vmem((ITERS, HALVES, n_zed, 2, rows, width), BF16),
            vmem((ITERS, HALVES, n_src, rows, width), BF16),
            sems((chunks,)),
            sems((2, 2)),
            sems,
            sems,
            sems,
            sems,
            sems((ITERS, HALVES)),
            sems((ITERS, HALVES)),
            sems((ITERS, HALVES)),
            sems((ITERS, HALVES)),
            sems((ITERS, HALVES)),
            sems((ITERS, HALVES)),
        ],
        compiler_params=pltpu.CompilerParams(
            collective_id=0, has_side_effects=True, vmem_limit_bytes=52 << 20
        ),
        name="predict",
    )(
        table,
        small,
        traces.reshape(block_rows * shot_local, samples),
        data,
    )
    shape = (rows, 2, shots)
    return multiples.reshape(shape), primaries.reshape(shape)


def solution(mesh):
    in_specs = (P("row", "src", None), P("row"), P(None, "row", None, "src"), P())
    out_specs = (P(("row", "src"), None, None), P(("row", "src"), None, None))
    return jax.shard_map(body, mesh=mesh, in_specs=in_specs, out_specs=out_specs, check_vma=False)
```

```python
import contextlib
import functools

import jax
import jax.numpy as jnp
from jax import lax
from jax.experimental import pallas as pl
from jax.experimental.pallas import tpu as pltpu
from jax.sharding import PartitionSpec as P

FREQ = 61
ITERS = 3
HALVES = 2
NEAR = 4
SIDES = (4, 4)
MESH = pl.DeviceIdType.MESH
F32, BF16 = jnp.float32, jnp.bfloat16


def dft_kernel(samples, lines):
    ticks, line = iota((lines, samples), 1), iota((lines, samples), 0)
    moment = ticks.astype(jnp.float32)
    ramp_len = samples // 8
    rising = 0.5 - 0.5 * jnp.cos(jnp.pi * (moment + 0.5) / ramp_len)
    falling = 0.5 - 0.5 * jnp.cos(jnp.pi * (samples - moment - 0.5) / ramp_len)
    taper = jnp.where(
        ticks < ramp_len,
        rising,
        jnp.where(ticks >= samples - ramp_len, falling, jnp.ones_like(rising)),
    )
    wrapped = ticks * FREQ % samples
    angles = 2.0 * jnp.pi / samples * wrapped.astype(jnp.float32)
    factor = 1.0 / jnp.sqrt(jnp.float32(samples))
    table = jnp.where(line == 0, taper * jnp.cos(angles) * factor, -taper * jnp.sin(angles) * factor)
    return table.astype(BF16).astype(F32)


def stage(name):
    return contextlib.nullcontext()


def log2(n):
    assert n & (n - 1) == 0, n
    return n.bit_length() - 1


def iota(shape, axis):
    return lax.broadcasted_iota(jnp.int32, shape, axis)


def predict(
    sizes, table_ref, small_ref, traces_ref, data_ref, mult_ref, prim_ref,
    traces, staged, estimate, first, spread, place, chosen, spectra, arrived, packed, pieces,
    base, gathered, whole, sent, came,
    tr_sem, load_sem, a_send, a_recv, b_send, b_recv,
    ag_send, ag_recv, ag_other, ag_beside, rs_send, rs_recv,
):
    n_row, n_src, rows, shot_local, sides = sizes
    n_zed = n_src // 2
    row, src = lax.axis_index("row"), lax.axis_index("src")
    zed, core = lax.div(src, 2), lax.rem(src, 2)
    block_rows = rows * n_src
    group = block_rows // n_row
    depth = n_row * rows
    shots = n_src * shot_local
    per_half = shots // HALVES
    chunks, chunk = traces.shape[0], traces.shape[1]
    packs = rows // group

    def trace_copy(k):
        return pltpu.make_async_copy(traces_ref.at[pl.ds(k * chunk, chunk)], traces.at[k], tr_sem.at[k])

    ahead = 4
    for k in range(ahead):
        trace_copy(k).start()

    loads = [
        pltpu.make_async_copy(data_ref.at[c, :, z], staged.at[c, z], load_sem.at[c, z]) for c in range(2) for z in range(2)
    ]

    lanes = 8 * shot_local
    from_lane, to_lane = iota((2 * lanes, lanes), 0), iota((2 * lanes, lanes), 1)
    same = (from_lane >> log2(lanes) == (to_lane >> log2(shot_local) & 1)) & (
        (from_lane ^ to_lane) & (shot_local - 1) == 0
    )
    spread[...] = jnp.where(same, 1.0, 0.0).astype(BF16)
    samples = table_ref.shape[1]
    table_row = iota((16, samples), 0)
    table = jnp.where(table_row == 0, table_ref[0:1], jnp.where(table_row == 1, table_ref[1:2], 0.0)).astype(BF16)
    own_lanes = iota((8, lanes), 1) >> log2(shot_local) == iota((8, lanes), 0)

    barrier = pltpu.get_barrier_semaphore()

    @pl.loop(1, n_row)
    def _(k):
        pl.semaphore_signal(barrier, inc=1, device_id=(lax.rem(row + k, n_row), src), device_id_type=MESH)

    @pl.loop(1, n_src)
    def _(k):
        pl.semaphore_signal(barrier, inc=1, device_id=(row, lax.rem(src + k, n_src)), device_id_type=MESH)

    for k in range(chunks):
        with stage("trace wait"):
            trace_copy(k).wait()

        if k + ahead < chunks:
            trace_copy(k + ahead).start()
        if k + ahead == chunks:
            for load in loads:
                load.start()

        spectrum = lax.dot_general(
            table, traces[k], (((1,), (1,)), ((), ())), preferred_element_type=F32
        )
        parts = []
        for c in range(2):
            pieces_of = [
                jnp.where(own_lanes, jnp.broadcast_to(spectrum[c : c + 1, g : g + lanes], (8, lanes)), 0.0)
                for g in range(0, chunk, lanes)
            ]
            parts.append(jnp.concatenate(pieces_of, axis=0).astype(BF16))
        block = jnp.dot(jnp.concatenate(parts, axis=1), spread[...], preferred_element_type=F32)
        block = block.astype(BF16).reshape(-1, group, lanes)
        groups = block.shape[0]
        spectra[k * groups : (k + 1) * groups] = block

    with stage("barrier"):
        pl.semaphore_wait(barrier, n_row - 1 + n_src - 1)

    def to_row(k):
        target = lax.rem(row + k, n_row)
        return pltpu.make_async_remote_copy(
            src_ref=spectra.at[target],
            dst_ref=arrived.at[row],
            send_sem=a_send,
            recv_sem=a_recv,
            device_id=(target, src),
            device_id_type=MESH,
        )

    @pl.loop(1, n_row)
    def _(k):
        to_row(k).start()

    arrived[row] = spectra[row]

    where = small_ref[:, :block_rows].astype(jnp.int32)
    located = (where >> log2(block_rows)) * group + (where & (group - 1))
    width = 256
    for at in range(0, block_rows, width):
        hit = iota((block_rows, width), 0) == jnp.broadcast_to(located[:, at : at + width], (block_rows, width))
        turned = jnp.where(hit, 1.0, 0.0).astype(BF16).T
        for u in range(0, width, group):
            device, pack = (at + u) // rows, (at + u) % rows // group
            to = (pack * n_src + device) * group
            chosen[to : to + group, :] = turned[u : u + group, :]

    from_lane, to_lane = iota((n_src * lanes, 2 * shots), 0), iota((n_src * lanes, 2 * shots), 1)
    shot = (from_lane >> log2(lanes)) * shot_local + (from_lane & (shot_local - 1))
    imag = from_lane >> log2(shot_local) & 1
    goal = (shot >> log2(per_half)) * (2 * per_half) + imag * per_half + (shot & (per_half - 1))
    place[...] = jnp.where(goal == to_lane, 1.0, 0.0).astype(BF16)

    def wait_for(ref, count, sem):
        pltpu.make_async_copy(ref.at[pl.ds(0, count)], ref.at[pl.ds(0, count)], sem).wait()

    with stage("row wait"):
        wait_for(arrived, n_row - 1, a_recv)
    ordered = jnp.dot(
        chosen[...], arrived[...].reshape(block_rows, lanes), preferred_element_type=F32
    ).reshape(packs, n_src * group, lanes)
    own_pack = iota((n_src * group, lanes), 1) >> log2(2 * shot_local)
    joined = jnp.zeros((n_src * group, lanes), F32)
    for p in range(packs):
        joined = jnp.where(own_pack == p, ordered[p], joined)
    packed[...] = joined.astype(BF16).reshape(n_src, group, lanes)

    def to_src(k):
        target = lax.rem(src + k, n_src)
        return pltpu.make_async_remote_copy(
            src_ref=packed.at[target],
            dst_ref=pieces.at[src],
            send_sem=b_send,
            recv_sem=b_recv,
            device_id=(row, target),
            device_id_type=MESH,
        )

    @pl.loop(1, n_src)
    def _(k):
        to_src(k).start()

    pieces[src] = packed[src]

    for load in loads:
        load.wait()

    with stage("src wait"):
        wait_for(pieces, n_src - 1, b_recv)
    lane_pack = iota((group, lanes), 1) >> log2(2 * shot_local)
    left = []
    for s in range(n_src):
        piece = pieces[s].astype(F32)
        left.append(
            jnp.concatenate([jnp.where(lane_pack == p, piece, 0.0) for p in range(packs)], axis=0).astype(BF16)
        )
    panel = jnp.dot(jnp.concatenate(left, axis=1), place[...], preferred_element_type=F32)

    side_x, side_y = sides
    along_x, along_y, along_z = row // (2 * side_y), row // 2 % side_y, row % 2
    plane = side_x * side_y
    beside = row + 1 - 2 * along_z
    other_z = 1 - along_z
    slot = along_z * plane + row // 2
    slot_beside = other_z * plane + row // 2

    def away(x, y):
        return min(x, side_x - x) + min(y, side_y - y)

    offsets = [(x, y) for x in range(side_x) for y in range(side_y) if x or y]
    offsets.sort(key=lambda o: -away(*o))
    far = [o for o in offsets if away(*o) > NEAR]
    near = [o for o in offsets if away(*o) <= NEAR]

    def send_block(it, h, which, target, sem):
        return pltpu.make_async_remote_copy(
            src_ref=gathered.at[it, h, which],
            dst_ref=gathered.at[it, h, which],
            send_sem=ag_send.at[it, h],
            recv_sem=sem.at[it, h],
            device_id=(target, src),
            device_id_type=MESH,
        )

    def send_over(it, h, which, chips, to_z, sem):
        for x, y in chips:
            to_x = lax.rem(along_x + side_x + x - 2 * core * x + core * side_x, side_x)
            to_y = lax.rem(along_y + side_y + y - 2 * core * y + core * side_y, side_y)
            send_block(it, h, which, (to_x * side_y + to_y) * 2 + to_z, sem).start()

    def share(it, h, value):
        gathered[it, h, slot] = value.astype(BF16)
        send_block(it, h, slot, beside, ag_beside).start()
        send_over(it, h, slot, far, other_z, ag_other)
        send_over(it, h, slot, offsets, along_z, ag_recv)

    def relay(it, h):
        with stage("relay"):
            send_block(it, h, slot_beside, beside, ag_beside).wait_recv()
        send_over(it, h, slot_beside, near, along_z, ag_other)

    width = 2 * per_half
    for h in range(HALVES):
        base[h] = panel[:, h * width : (h + 1) * width]
        share(0, h, base[h])
        if h == 0:
            relay(0, 0)

    def to_owner(it, h, chip, c):
        return pltpu.make_async_remote_copy(
            src_ref=sent.at[it, h, chip, c],
            dst_ref=came.at[it, h, src],
            send_sem=rs_send.at[it, h],
            recv_sem=rs_recv.at[it, h],
            device_id=(row, chip * 2 + c),
            device_id_type=MESH,
        )

    sign = jnp.where(iota((1, width), 1) < per_half, -1.0, 1.0)

    def crossed(v):
        return pltpu.roll(v, per_half, 1) * sign

    def multiply(it, h):
        def terms_of(z, pair):
            columns = pl.ds(pl.multiple_of(pair * 4 * rows, 4 * rows), 4 * rows)
            real_terms, imag_terms = (
                jnp.dot(
                    estimate[h],
                    staged.at[c, z].reshape(depth // 2, block_rows)[:, columns],
                    preferred_element_type=F32,
                )
                for c in range(2)
            )
            real = real_terms[:per_half] - imag_terms[per_half:]
            imag = real_terms[per_half:] + imag_terms[:per_half]
            return jnp.concatenate([real, imag], axis=0)

        def turn(z):
            at = pl.multiple_of(z * plane, plane)
            estimate[h] = gathered.at[it, h, pl.ds(at, plane)].reshape(depth // 2, width)[...].T

        pairs = [lax.rem(zed // 2 + 1 + n, 2) for n in range(2)]
        with stage("plane wait"):
            wait_for(gathered.at[it, h], plane - 1, ag_recv.at[it, h])
        with stage("multiply plane"):
            turn(along_z)
            for n in range(2):
                first[n] = terms_of(along_z, pairs[n])
        with stage("gather wait"):
            wait_for(gathered.at[it, h], plane - 1, ag_other.at[it, h])
        with stage("multiply"):
            turn(other_z)
            for n, pair in enumerate(pairs):
                both = first[n] + terms_of(other_z, pair)
                sent[it, h, pl.ds(pair * 2, 2)] = both.astype(BF16).T.reshape(2, 2, rows, width)
                if n:
                    for c in range(2):
                        to_owner(it, h, zed + 1 - 2 * lax.rem(zed, 2), c).start()
                    to_owner(it, h, zed, 1 - core).start()
                    whole[h] = both.T.reshape(2, 2, rows, width)
                else:
                    for chip in range(2):
                        for c in range(2):
                            to_owner(it, h, pair * 2 + lax.rem(zed + chip, 2), c).start()

    wave_real, wave_imag = small_ref[:, block_rows : block_rows + 1], small_ref[:, block_rows + 1 : block_rows + 2]

    def finish(it, h):
        with stage("sum wait"):
            wait_for(came.at[it, h], n_src - 1, rs_recv.at[it, h])
        total = whole[h, lax.rem(zed, 2), core]
        for k in range(1, n_src):
            total = total + came[it, h, lax.rem(src + k, n_src)].astype(F32)
        return total, base[h] - (wave_real * total + wave_imag * crossed(total))

    @pl.loop(0, ITERS - 1)
    def _(it):
        for h in range(HALVES):
            multiply(it, h)
            relay(it + h, 1 - h)
            share(it + 1, h, finish(it, h)[1])

    multiply(ITERS - 1, 0)
    relay(ITERS - 1, 1)
    multiply(ITERS - 1, 1)
    for h in range(HALVES):
        total, primary = finish(ITERS - 1, h)
        for c in range(2):
            to = c * shots + h * per_half
            mult_ref[:, to : to + per_half] = total[:, c * per_half : (c + 1) * per_half]
            prim_ref[:, to : to + per_half] = primary[:, c * per_half : (c + 1) * per_half]

    wait_for(spectra, n_row - 1, a_send)
    wait_for(packed, n_src - 1, b_send)

    @pl.loop(0, ITERS)
    def _(it):
        for h in range(HALVES):
            wait_for(gathered.at[it, h], n_row - 1, ag_send.at[it, h])
            wait_for(came.at[it, h], n_src - 1, rs_send.at[it, h])


def body(traces, row_source, slice_data, wavelet_inverse):
    block_rows, shot_local, samples = traces.shape
    n_row, n_src = lax.axis_size("row"), lax.axis_size("src")
    n_zed = n_src // 2
    rows = block_rows // n_src
    group = block_rows // n_row
    shots = n_src * shot_local
    depth = n_row * rows
    width = 2 * shots // HALVES
    lanes = 8 * shot_local
    chunk = 1024
    chunks = block_rows * shot_local // chunk
    lines = 8
    small = jnp.pad(row_source, (0, 128)).astype(F32) + jnp.pad(wavelet_inverse, (block_rows, 126))
    small = small.reshape(1, -1)
    table = dft_kernel(samples, lines)
    data = jnp.transpose(slice_data, (0, 2, 3, 1)).reshape(2, n_row // 2, 2, rows, block_rows)
    block = jax.ShapeDtypeStruct((rows, 2 * shots), F32)
    vmem, sems = pltpu.VMEM, pltpu.SemaphoreType.DMA
    multiples, primaries = pl.pallas_call(
        functools.partial(predict, (n_row, n_src, rows, shot_local, SIDES)),
        out_shape=(block, block),
        in_specs=[
            pl.BlockSpec(memory_space=pltpu.VMEM),
            pl.BlockSpec(memory_space=pltpu.VMEM),
            pl.BlockSpec(memory_space=pltpu.HBM),
            pl.BlockSpec(memory_space=pltpu.HBM),
        ],
        out_specs=(pl.BlockSpec(memory_space=pltpu.VMEM),) * 2,
        scratch_shapes=[
            vmem((chunks, chunk, samples), BF16),
            vmem((2, 2, n_row // 2, rows, block_rows), BF16),
            vmem((HALVES, width, depth // 2), BF16),
            vmem((2, width, 4 * rows), F32),
            vmem((2 * lanes, lanes), BF16),
            vmem((n_src * lanes, 2 * shots), BF16),
            vmem((block_rows, block_rows), BF16),
            vmem((n_row, group, lanes), BF16),
            vmem((n_row, group, lanes), BF16),
            vmem((n_src, group, lanes), BF16),
            vmem((n_src, group, lanes), BF16),
            vmem((HALVES, rows, width), F32),
            vmem((ITERS, HALVES, n_row, rows, width), BF16),
            vmem((HALVES, 2, 2, rows, width), F32),
            vmem((ITERS, HALVES, n_zed, 2, rows, width), BF16),
            vmem((ITERS, HALVES, n_src, rows, width), BF16),
            sems((chunks,)),
            sems((2, 2)),
            sems,
            sems,
            sems,
            sems,
            sems((ITERS, HALVES)),
            sems((ITERS, HALVES)),
            sems((ITERS, HALVES)),
            sems((ITERS, HALVES)),
            sems((ITERS, HALVES)),
            sems((ITERS, HALVES)),
        ],
        compiler_params=pltpu.CompilerParams(
            collective_id=0, has_side_effects=True, vmem_limit_bytes=52 << 20
        ),
        name="predict",
    )(
        table,
        small,
        traces.reshape(block_rows * shot_local, samples),
        data,
    )
    shape = (rows, 2, shots)
    return multiples.reshape(shape), primaries.reshape(shape)


def solution(mesh):
    in_specs = (P("row", "src", None), P("row"), P(None, "row", None, "src"), P())
    out_specs = (P(("row", "src"), None, None), P(("row", "src"), None, None))
    return jax.shard_map(body, mesh=mesh, in_specs=in_specs, out_specs=out_specs, check_vma=False)
```
